32 devices in a mesh: dp: 2 (over x), expert: 16 (over z, y, core).
Axes of the slice: x: 2, y: 2, z: 4, core: 2. Of those that a mesh axis runs over, the one named last changes fastest.
Arguments:
- tokens: bfloat16 [4096, 2048], P(('dp', 'expert')), may hold values from -6 to 6
- gate_weights: float32 [4096, 2], P(('dp', 'expert')), may hold values from 0.02 to 0.5
- expert_ids: int32 [4096, 2], P(('dp', 'expert')), may hold values from 0 to 15, as said below
- hot_experts: int32 [4], replicated, may hold values from 0 to 15, as said below
- gate_proj: bfloat16 [16, 2048, 768], P('expert', 'dp'), may hold values from -0.125 to 0.125
- up_proj: bfloat16 [16, 2048, 768], P('expert', 'dp'), may hold values from -0.125 to 0.125
- down_proj: bfloat16 [16, 2048, 768], P('expert', 'dp'), may hold values from -0.21875 to 0.21875
- out_grad: bfloat16 [4096, 2048], P(('dp', 'expert')), may hold values from -6 to 6
Outputs:
- layer_out: bfloat16 [4096, 2048], P(('dp', 'expert'))
- tokens_grad: bfloat16 [4096, 2048], P(('dp', 'expert'))
- routing_grad: float32 [4096, 2], P(('dp', 'expert'))
- gate_proj_grad: bfloat16 [16, 2048, 768], P('expert', 'dp')
- up_proj_grad: bfloat16 [16, 2048, 768], P('expert', 'dp')
- down_proj_grad: bfloat16 [16, 2048, 768], P('expert', 'dp')
The draws below stay inside these ranges and needn't reach their ends.
Inputs may be any that keep to these rules, and one draw needn't show every extreme that they name: `expert_ids`: each token names 2 different experts. In each block of 128 rows of one device no expert is named more than 28 times, and the expert hot_experts[0] is named exactly 28 times in every block. `hot_experts`: 4 different experts.
All inputs are finite; a program needn't handle non-finite values.
Results may differ from the reference program's by a relative error of at most 0.012.
Values may be sent and summed in bfloat16 or wider, within the bound.
No kernel may reach another device: no remote copies, remote signals or barrier semaphores. Data moves between devices by JAX's collectives and lax.ppermute only.
A program may use at most 128 MiB of HBM per device.

```python
import math
import jax
import jax.numpy as jnp
from jax import lax

D = 2048
FF = 768
TOPK = 2
HOT = 4
TOK_DEV = 128
EXPERTS = 16
CAP = 20
SLOTS = 28
TOKENS = 4096
N_DP = 2
N_EXPERT = 16


def token_shuffle(sub_key):
    return jax.random.permutation(sub_key, TOK_DEV)


def routing_draw(key):
    blocks = TOKENS // TOK_DEV
    assigned = TOK_DEV * TOPK
    shuffled = jax.random.permutation(jax.random.fold_in(key, 17), EXPERTS).astype(jnp.int32)
    last_expert = EXPERTS - 1
    rank_index = jnp.arange(EXPERTS, dtype=jnp.int32)
    last_place = jnp.sum(jnp.where(shuffled == last_expert, rank_index, 0)).astype(jnp.int32)
    expert_order = shuffled.at[last_place].set(shuffled[1]).at[1].set(last_expert)
    remain = assigned - SLOTS
    others = EXPERTS - 1
    low_load = remain // others
    spare_count = remain % others
    high_load = low_load + min(spare_count, 1)
    reach_most = min(low_load, SLOTS - high_load)
    base_load = jnp.where(rank_index == 0, SLOTS, low_load + (rank_index - 1 < spare_count).astype(jnp.int32)).astype(jnp.int32)
    couples = others // 2
    load_moves = jax.random.randint(jax.random.fold_in(key, 23), (blocks, couples), 0, reach_most + 1, dtype=jnp.int32)
    change = jnp.zeros((blocks, EXPERTS), jnp.int32)
    change = change.at[:, 1:2 * couples:2].add(load_moves)
    change = change.at[:, 2:2 * couples + 1:2].add(-load_moves)
    ranked_load = base_load[None, :] + change
    block_loads = jnp.zeros((blocks, EXPERTS), jnp.int32).at[:, expert_order].set(ranked_load)
    load_ends = jnp.cumsum(block_loads, axis=1)
    entries = jnp.arange(assigned, dtype=jnp.int32)
    chosen = jnp.sum((load_ends[:, None, :] <= entries[None, :, None]).astype(jnp.int32), axis=2)
    id_table = jnp.transpose(chosen.reshape(blocks, TOPK, TOK_DEV), (0, 2, 1))
    token_keys = jax.random.split(jax.random.fold_in(key, 29), blocks)
    token_order = jax.vmap(token_shuffle)(token_keys).astype(jnp.int32)
    id_table = jnp.take_along_axis(id_table, token_order[:, :, None], axis=1)
    scores = jax.random.randint(jax.random.fold_in(key, 31), (blocks, TOK_DEV, TOPK), 0, 1048576, dtype=jnp.int32) * TOPK + jnp.arange(TOPK, dtype=jnp.int32)
    slot_order = jnp.argsort(scores, axis=2, stable=True).astype(jnp.int32)
    id_table = jnp.take_along_axis(id_table, slot_order, axis=2)
    return (id_table.reshape(TOKENS, TOPK).astype(jnp.int32), expert_order)


def draw_expert_ids(key, part):
    id_table, expert_order = routing_draw(key)
    return id_table


def draw_hot_experts(key, part):
    id_table, expert_order = routing_draw(key)
    pick_ranks = jnp.array([0] + [2 * member + 1 for member in range(HOT - 1)], dtype=jnp.int32)
    return expert_order[pick_ranks]


def shard_levels(stream_key, dims, pieces, least, largest):
    level, own = 1.0, jax.random.fold_in(stream_key, 6)
    for position, blocks in pieces:
        draws = jnp.exp(jax.random.uniform(jax.random.fold_in(own, position), (blocks,), jnp.float32, least / len(pieces), largest / len(pieces)))
        level = level * jnp.repeat(draws, dims[position] // blocks).reshape([-1 if axis == position else 1 for axis in range(len(dims))])
    return level


def scatter_about(own_key, extent, spread, most, shards=(), held_as=jnp.bfloat16):
    gain = shard_levels(own_key, extent, shards, -0.22, 0.18) if shards else 1.0
    drawn = jax.random.normal(own_key, extent, jnp.float32) * spread * gain
    return jnp.minimum(jnp.maximum(drawn, -most), most).astype(held_as)


def setup_inputs(seed: int = 0) -> dict:
    splits = jax.random.split(jax.random.key(seed), 9)
    return {
        "tokens": scatter_about(splits[0], (TOKENS, D), 1.0, 6.0, ((0, 32),)),
        "gate_weights": jnp.clip(jnp.exp(math.log(0.5) - 3.218876 * jax.random.uniform(splits[1], (TOKENS, TOPK), jnp.float32) ** shard_levels(splits[1], (TOKENS, TOPK), ((0, 32),), -0.2, 0.2)), 0.02, 0.5),
        "expert_ids": draw_expert_ids(jax.random.fold_in(splits[8], 71), 0),
        "hot_experts": draw_hot_experts(jax.random.fold_in(splits[8], 71), 0),
        "gate_proj": scatter_about(splits[4], (EXPERTS, D, FF), D ** -0.5, 0.125, ((0, 16), (1, 2))),
        "up_proj": scatter_about(splits[5], (EXPERTS, D, FF), D ** -0.5, 0.125, ((0, 16), (1, 2))),
        "down_proj": scatter_about(splits[6], (EXPERTS, D, FF), FF ** -0.5, 0.21875, ((0, 16), (1, 2))),
        "out_grad": scatter_about(splits[7], (TOKENS, D), 1.0, 6.0, ((0, 32),)),
    }


def split_sums(left_side, right_side):
    left_split = left_side.reshape(N_DP, -1, left_side.shape[1]).astype(jnp.float32)
    right_split = right_side.reshape(N_DP, -1, right_side.shape[1]).astype(jnp.float32)
    products = jnp.einsum("nrd,nrf->ndf", left_split, right_split, precision=lax.Precision.HIGHEST)
    rounded = lax.optimization_barrier(products.astype(jnp.bfloat16))
    return jnp.sum(rounded.astype(jnp.float32), axis=0).astype(jnp.bfloat16)


def contract_last(left_side, right_side):
    return lax.dot_general(left_side, right_side, (((1,), (1,)), ((), ())), preferred_element_type=jnp.float32)


def reference(tokens, gate_weights, expert_ids, hot_experts, gate_proj, up_proj, down_proj, out_grad):
    blocks = tokens.shape[0] // TOK_DEV
    model_width = tokens.shape[1]
    assigned = TOK_DEV * TOPK
    flat_ids = expert_ids.reshape(blocks, assigned)
    expert_range = jnp.arange(EXPERTS, dtype=jnp.int32)
    onehot = (flat_ids[:, :, None] == expert_range[None, None, :]).astype(jnp.int32)
    before = jnp.cumsum(onehot, axis=1) - onehot
    slot_pos = jnp.sum(before * onehot, axis=2)
    hot_flags = jnp.sum((hot_experts[:, None] == expert_range[None, :]).astype(jnp.int32), axis=0)
    hot_row = jnp.sum(onehot * hot_flags[None, None, :], axis=2) > 0
    kept_mask = slot_pos < jnp.where(hot_row, SLOTS, CAP)
    block_index = jnp.arange(blocks, dtype=jnp.int32)[:, None]
    token_index = block_index * TOK_DEV + jnp.arange(assigned, dtype=jnp.int32)[None, :] // TOPK
    table_size = blocks * EXPERTS * SLOTS
    target = jnp.where(kept_mask, (block_index * EXPERTS + flat_ids) * SLOTS + slot_pos, table_size)
    source_row = jnp.full((table_size + 1,), tokens.shape[0], jnp.int32).at[target.reshape(-1)].set(token_index.reshape(-1))
    source_weight = jnp.zeros((table_size + 1,), jnp.float32).at[target.reshape(-1)].set(gate_weights.reshape(-1))
    source_row = source_row[:table_size].reshape(N_DP, N_EXPERT, EXPERTS, SLOTS)
    source_weight = source_weight[:table_size].reshape(N_DP, N_EXPERT, EXPERTS, SLOTS)
    padded_tokens = jnp.concatenate([tokens, jnp.zeros((1, model_width), jnp.bfloat16)], axis=0)
    padded_grad = jnp.concatenate([out_grad, jnp.zeros((1, model_width), jnp.bfloat16)], axis=0)

    def per_expert(expert_id):
        row_ids = jnp.take(source_row, expert_id, axis=2).reshape(-1)
        row_weight = jnp.take(source_weight, expert_id, axis=2).reshape(-1, 1)
        expert_rows = padded_tokens[row_ids]
        grad_in = (row_weight * padded_grad[row_ids].astype(jnp.float32)).astype(jnp.bfloat16)
        local_gate = gate_proj[expert_id]
        local_up = up_proj[expert_id]
        local_down = down_proj[expert_id]
        gate_act = jnp.dot(expert_rows, local_gate, preferred_element_type=jnp.float32)
        up_act = jnp.dot(expert_rows, local_up, preferred_element_type=jnp.float32)
        sigmoid_act = jax.nn.sigmoid(gate_act)
        silu_act = gate_act * sigmoid_act
        hidden = (silu_act * up_act).astype(jnp.bfloat16)
        output = contract_last(hidden, local_down).astype(jnp.bfloat16)
        grad_hidden = jnp.dot(grad_in, local_down, preferred_element_type=jnp.float32)
        grad_up = (grad_hidden * silu_act).astype(jnp.bfloat16)
        grad_gate = (grad_hidden * up_act * sigmoid_act * (1.0 + gate_act * (1.0 - sigmoid_act))).astype(jnp.bfloat16)
        grad_rows = (contract_last(grad_gate, local_gate) + contract_last(grad_up, local_up)).astype(jnp.bfloat16)
        gate_sum = split_sums(expert_rows, grad_gate)
        up_sum = split_sums(expert_rows, grad_up)
        down_sum = split_sums(grad_in, hidden)
        return output, grad_rows, gate_sum, up_sum, down_sum

    outputs, grad_rows, gate_proj_grad, up_proj_grad, down_proj_grad = lax.map(per_expert, expert_range)
    dp_index = block_index // N_EXPERT
    column = block_index % N_EXPERT
    row_at = (((flat_ids * N_DP + dp_index) * N_EXPERT + column) * SLOTS + jnp.minimum(slot_pos, SLOTS - 1)).reshape(-1)
    keep_scale = kept_mask.reshape(-1, 1).astype(jnp.float32)
    chosen = jnp.take(outputs.reshape(-1, model_width), row_at, axis=0).astype(jnp.float32) * keep_scale
    weight_flat = gate_weights.reshape(-1, 1)
    layer_out = (chosen * weight_flat).reshape(-1, TOPK, model_width).sum(axis=1).astype(jnp.bfloat16)
    routing_grad = jnp.sum(chosen.reshape(-1, TOPK, model_width) * out_grad.astype(jnp.float32)[:, None, :], axis=2)
    chosen_grad = jnp.take(grad_rows.reshape(-1, model_width), row_at, axis=0).astype(jnp.float32) * keep_scale
    tokens_grad = chosen_grad.reshape(-1, TOPK, model_width).sum(axis=1).astype(jnp.bfloat16)
    return layer_out, tokens_grad, routing_grad, gate_proj_grad, up_proj_grad, down_proj_grad
```

```python
import jax
import jax.numpy as jnp
from jax import lax
from jax.sharding import PartitionSpec as P

TOPK = 2
AXES = ("dp", "expert")


def contract_last(left_side, right_side):
    return lax.dot_general(
        left_side, right_side, (((1,), (1,)), ((), ())), preferred_element_type=jnp.float32
    )


def contract_first(left_side, right_side):
    return lax.dot_general(
        left_side, right_side, (((0,), (0,)), ((), ())), preferred_element_type=jnp.float32
    )


def dot(left_side, right_side):
    return jnp.dot(left_side, right_side, preferred_element_type=jnp.float32)


def make_body(n_dp, n_ex):
    def physical(v, e):
        return ((v >> 1) * 2 + (e & 1)) * n_ex + (e >> 1) * 2 + (v & 1)

    def move(value, where):
        pairs = [
            (physical(v, e), physical(*where(v, e))) for v in range(n_dp) for e in range(n_ex)
        ]
        return lax.ppermute(value, AXES, pairs)

    def transpose(value):
        pairs = [
            (i * n_ex + c, ((i & ~1) | (c & 1)) * n_ex + ((c & ~1) | (i & 1)))
            for i in range(n_dp)
            for c in range(n_ex)
        ]
        return lax.ppermute(value, AXES, pairs)

    half = n_ex // 2

    def across(value):
        return move(value, lambda v, e: (v, e ^ half))

    def to_owner(value, d):
        return move(value, lambda v, e: (v, e ^ d))

    def to_part(value, s):
        return move(value, lambda v, e: (v ^ s, e))

    def body(
        tokens, gate_weights, expert_ids, hot_experts, gate_proj, up_proj, down_proj, out_grad
    ):
        token_count, model_width = tokens.shape
        width = model_width // n_dp
        assign_count = token_count * TOPK
        cap_rows = 5 * assign_count // (4 * n_ex)
        slot_count = cap_rows + assign_count // (2 * n_ex)
        i_index = lax.axis_index("dp")
        c_index = lax.axis_index("expert")
        v_index = (i_index >> 1) * 2 + (c_index & 1)
        e_index = (c_index >> 1) * 2 + (i_index & 1)

        def turn(value):
            cols = [value[:, s * width : (s + 1) * width] for s in range(n_dp)]
            turned = []
            for s in range(n_dp):
                pick = cols[s]
                for j in range(n_dp):
                    if j != s:
                        pick = jnp.where(v_index == (j ^ s), cols[j], pick)
                turned.append(pick)
            return jnp.concatenate(turned, axis=1)

        tok = turn(tokens)
        og = turn(out_grad)
        tok_two = jnp.concatenate([tok, across(tok)], axis=0)
        og_two = jnp.concatenate([og, across(og)], axis=0)

        def gathered(shard):
            own = transpose(shard[0])
            return [own] + [to_part(own, s) for s in range(1, n_dp)]

        gate_parts = gathered(gate_proj)
        up_parts = gathered(up_proj)
        down_parts = gathered(down_proj)

        ids = expert_ids.T
        order = jnp.arange(token_count, dtype=jnp.int32)[None, :] * TOPK + jnp.arange(
            TOPK, dtype=jnp.int32
        )[:, None]
        flat_ids = ids.reshape(-1)
        flat_order = order.reshape(-1)
        same = (flat_ids[:, None] == flat_ids[None, :]) & (
            flat_order[:, None] < flat_order[None, :]
        )
        slot_pos = jnp.sum(same.astype(jnp.int32), axis=0)
        hot_row = jnp.any(flat_ids[None, :] == hot_experts[:, None], axis=0)
        kept_mask = slot_pos < jnp.where(hot_row, slot_count, cap_rows)
        target = jnp.where(kept_mask, flat_ids * slot_count + slot_pos, -1)
        routes = jnp.concatenate(
            [target.astype(jnp.float32).reshape(TOPK, -1), gate_weights.T], axis=0
        )
        routes = jnp.concatenate([routes, across(routes)], axis=1)
        target_two = routes[:TOPK].astype(jnp.int32)
        weight_two = routes[TOPK:]

        row_count = half * 2 * slot_count
        row = jnp.arange(row_count, dtype=jnp.int32)
        row_d = row // (2 * slot_count)
        row_block = (row // slot_count) % 2
        row_slot = row % slot_count
        row_expert = (e_index // half) * half + ((e_index % half) ^ row_d)
        row_code = row_expert * slot_count + row_slot
        col_block = jnp.arange(2 * token_count, dtype=jnp.int32) // token_count
        row_code = row_code[:, None]
        col_ok = row_block[:, None] == col_block[None, :]
        hits = [(row_code == target_two[k][None, :]) & col_ok for k in range(TOPK)]
        placing = (hits[0] | hits[1]).astype(jnp.bfloat16)
        weighted = jnp.where(
            hits[0], weight_two[0][None, :], jnp.where(hits[1], weight_two[1][None, :], 0.0)
        )
        row_weight = jnp.sum(weighted, axis=1, keepdims=True)
        weighted = weighted.astype(jnp.bfloat16)

        chunk = 2 * slot_count

        def exchange(rows):
            return jnp.concatenate(
                [rows[:chunk]]
                + [to_owner(rows[d * chunk : (d + 1) * chunk], d) for d in range(1, half)],
                axis=0,
            )

        expert_rows = exchange(dot(placing, tok_two).astype(jnp.bfloat16))
        grad_in = exchange((row_weight * dot(placing, og_two)).astype(jnp.bfloat16))

        def cols(value, s):
            return value[:, s * width : (s + 1) * width]

        def through(value, parts):
            total = dot(cols(value, 0), parts[0])
            for s in range(1, n_dp):
                total = total + dot(cols(value, s), parts[s])
            return total

        gate_act = through(expert_rows, gate_parts)
        up_act = through(expert_rows, up_parts)
        sigmoid_act = jax.nn.sigmoid(gate_act)
        silu_act = gate_act * sigmoid_act
        hidden = (silu_act * up_act).astype(jnp.bfloat16)
        output = jnp.concatenate(
            [contract_last(hidden, part).astype(jnp.bfloat16) for part in down_parts], axis=1
        )
        returned = exchange(output)

        grad_hidden = through(grad_in, down_parts)
        grad_up = (grad_hidden * silu_act).astype(jnp.bfloat16)
        grad_gate = (
            grad_hidden * up_act * sigmoid_act * (1.0 + gate_act * (1.0 - sigmoid_act))
        ).astype(jnp.bfloat16)
        grad_rows = jnp.concatenate(
            [
                (
                    contract_last(grad_gate, gate_parts[s]) + contract_last(grad_up, up_parts[s])
                ).astype(jnp.bfloat16)
                for s in range(n_dp)
            ],
            axis=1,
        )
        grad_back = exchange(grad_rows)

        def weight_grad(left_side, right_side):
            total = contract_first(cols(left_side, 0), right_side)
            for s in range(1, n_dp):
                term = contract_first(cols(left_side, s), right_side).astype(jnp.bfloat16)
                total = total + to_part(term, s).astype(jnp.float32)
            return transpose(total.astype(jnp.bfloat16))[None]

        down_proj_grad = weight_grad(grad_in, hidden)
        gate_proj_grad = weight_grad(expert_rows, grad_gate)
        up_proj_grad = weight_grad(expert_rows, grad_up)

        def join(part):
            own, other = part[:token_count], part[token_count:]
            return turn(
                (own + across(other.astype(jnp.bfloat16)).astype(jnp.float32)).astype(jnp.bfloat16)
            )

        layer_out = join(contract_first(weighted, returned))
        tokens_grad = join(contract_first(placing, grad_back))
        inner = contract_last(returned, og_two)
        routing = jnp.stack([jnp.sum(jnp.where(hit, inner, 0.0), axis=0) for hit in hits])
        routing_grad = (routing[:, :token_count] + across(routing[:, token_count:])).T
        return (layer_out, tokens_grad, routing_grad, gate_proj_grad, up_proj_grad, down_proj_grad)

    return body


def solution(mesh):
    in_specs = (
        P(("dp", "expert"), None),
        P(("dp", "expert"), None),
        P(("dp", "expert"), None),
        P(),
        P("expert", "dp", None),
        P("expert", "dp", None),
        P("expert", "dp", None),
        P(("dp", "expert"), None),
    )
    out_specs = (
        P(("dp", "expert"), None),
        P(("dp", "expert"), None),
        P(("dp", "expert"), None),
        P("expert", "dp", None),
        P("expert", "dp", None),
        P("expert", "dp", None),
    )
    body = make_body(mesh.shape["dp"], mesh.shape["expert"])
    return jax.shard_map(body, mesh=mesh, in_specs=in_specs, out_specs=out_specs, check_vma=False)
```

```python
import jax
import jax.numpy as jnp
from jax import lax
from jax.sharding import PartitionSpec as P


TOPK = 2
AXES = ("dp", "expert")


def contract_last(left_side, right_side):
    return lax.dot_general(
        left_side, right_side, (((1,), (1,)), ((), ())), preferred_element_type=jnp.float32
    )


def contract_first(left_side, right_side):
    return lax.dot_general(
        left_side, right_side, (((0,), (0,)), ((), ())), preferred_element_type=jnp.float32
    )


def dot(left_side, right_side):
    return jnp.dot(left_side, right_side, preferred_element_type=jnp.float32)


def make_body(n_dp, n_ex):
    def physical(v, e):
        return ((v >> 1) * 2 + (e & 1)) * n_ex + (e >> 1) * 2 + (v & 1)

    def move(value, where):
        pairs = [
            (physical(v, e), physical(*where(v, e))) for v in range(n_dp) for e in range(n_ex)
        ]
        return lax.ppermute(value, AXES, pairs)

    def transpose(value):
        pairs = [
            (i * n_ex + c, ((i & ~1) | (c & 1)) * n_ex + ((c & ~1) | (i & 1)))
            for i in range(n_dp)
            for c in range(n_ex)
            if (i & 1) != (c & 1)
        ]
        moved = lax.ppermute(value, AXES, pairs)
        stays = (lax.axis_index("dp") & 1) == (lax.axis_index("expert") & 1)
        return lax.optimization_barrier(jnp.where(stays, value, moved))

    half = n_ex // 2

    def across(value):
        return move(value, lambda v, e: (v, e ^ half))

    def to_owner(value, d):
        return move(value, lambda v, e: (v, e ^ d))

    def to_part(value, s):
        return move(value, lambda v, e: (v ^ s, e))

    def body(
        tokens, gate_weights, expert_ids, hot_experts, gate_proj, up_proj, down_proj, out_grad
    ):
        token_count, model_width = tokens.shape
        width = model_width // n_dp
        assign_count = token_count * TOPK
        cap_rows = 5 * assign_count // (4 * n_ex)
        slot_count = cap_rows + assign_count // (2 * n_ex)
        i_index = lax.axis_index("dp")
        c_index = lax.axis_index("expert")
        v_index = (i_index >> 1) * 2 + (c_index & 1)
        e_index = (c_index >> 1) * 2 + (i_index & 1)

        def turn(value):
            cols = [value[:, s * width : (s + 1) * width] for s in range(n_dp)]
            turned = []
            for s in range(n_dp):
                pick = cols[s]
                for j in range(n_dp):
                    if j != s:
                        pick = jnp.where(v_index == (j ^ s), cols[j], pick)
                turned.append(pick)
            return jnp.concatenate(turned, axis=1)

        tok = turn(tokens)
        og = turn(out_grad)
        tok_far = across(tok)
        og_far = across(og)
        tok_two = jnp.concatenate([tok, tok_far], axis=0)
        og_two = jnp.concatenate([og, og_far], axis=0)

        def gathered(shard):
            own = transpose(shard[0])
            return [own] + [to_part(own, s) for s in range(1, n_dp)]

        gate_parts = gathered(gate_proj)
        up_parts = gathered(up_proj)
        down_parts = gathered(down_proj)

        ids = expert_ids.T
        order = jnp.arange(token_count, dtype=jnp.int32)[None, :] * TOPK + jnp.arange(
            TOPK, dtype=jnp.int32
        )[:, None]
        flat_ids = ids.reshape(-1)
        flat_order = order.reshape(-1)
        same = (flat_ids[:, None] == flat_ids[None, :]) & (
            flat_order[:, None] < flat_order[None, :]
        )
        slot_pos = jnp.sum(same.astype(jnp.int32), axis=0)
        hot_row = jnp.any(flat_ids[None, :] == hot_experts[:, None], axis=0)
        kept_mask = slot_pos < jnp.where(hot_row, slot_count, cap_rows)
        target = jnp.where(kept_mask, flat_ids * slot_count + slot_pos, -1)
        routes = jnp.concatenate(
            [target.astype(jnp.float32).reshape(TOPK, -1), gate_weights.T], axis=0
        )
        routes_far = across(routes)
        routes = jnp.concatenate([routes, routes_far], axis=1)
        target_two = routes[:TOPK].astype(jnp.int32)
        weight_two = routes[TOPK:]

        row_count = half * 2 * slot_count
        row = jnp.arange(row_count, dtype=jnp.int32)
        row_d = row // (2 * slot_count)
        row_block = (row // slot_count) % 2
        row_slot = row % slot_count
        row_expert = (e_index // half) * half + ((e_index % half) ^ row_d)
        row_code = row_expert * slot_count + row_slot
        col_block = jnp.arange(2 * token_count, dtype=jnp.int32) // token_count
        row_code = row_code[:, None]
        col_ok = row_block[:, None] == col_block[None, :]
        hits = [(row_code == target_two[k][None, :]) & col_ok for k in range(TOPK)]
        placing = (hits[0] | hits[1]).astype(jnp.bfloat16)
        weighted = jnp.where(
            hits[0], weight_two[0][None, :], jnp.where(hits[1], weight_two[1][None, :], 0.0)
        )
        row_weight = jnp.sum(weighted, axis=1, keepdims=True)
        placing, weighted, row_weight = lax.optimization_barrier(
            (placing, weighted.astype(jnp.bfloat16), row_weight)
        )

        chunk = 2 * slot_count

        def exchange(rows):
            pieces = [rows[d * chunk : (d + 1) * chunk] for d in range(half)]
            moved = [to_owner(pieces[d], d) for d in range(1, half)]
            return jnp.concatenate([pieces[0]] + moved, axis=0)

        tok_rows = dot(placing, tok_two).astype(jnp.bfloat16)
        og_rows = (row_weight * dot(placing, og_two)).astype(jnp.bfloat16)
        expert_rows = exchange(tok_rows)
        grad_in = exchange(og_rows)

        def cols(value, s):
            return value[:, s * width : (s + 1) * width]

        def through(value, parts):
            total = dot(cols(value, 0), parts[0])
            for s in range(1, n_dp):
                total = total + dot(cols(value, s), parts[s])
            return total

        gate_act = through(expert_rows, gate_parts)
        up_act = through(expert_rows, up_parts)
        hidden = (gate_act * jax.nn.sigmoid(gate_act) * up_act).astype(jnp.bfloat16)
        gate_act, up_act, hidden = lax.optimization_barrier((gate_act, up_act, hidden))
        output = jnp.concatenate(
            [contract_last(hidden, part).astype(jnp.bfloat16) for part in down_parts], axis=1
        )
        sigmoid_act = jax.nn.sigmoid(gate_act)
        silu_act = gate_act * sigmoid_act
        returned = exchange(output)

        grad_hidden = through(grad_in, down_parts)
        grad_up = (grad_hidden * silu_act).astype(jnp.bfloat16)
        grad_gate = (
            grad_hidden * up_act * sigmoid_act * (1.0 + gate_act * (1.0 - sigmoid_act))
        ).astype(jnp.bfloat16)
        grad_rows = jnp.concatenate(
            [
                (
                    contract_last(grad_gate, gate_parts[s]) + contract_last(grad_up, up_parts[s])
                ).astype(jnp.bfloat16)
                for s in range(n_dp)
            ],
            axis=1,
        )
        grad_back = exchange(grad_rows)

        def weight_grad(left_side, right_side):
            terms = [
                contract_first(cols(left_side, s), right_side).astype(jnp.bfloat16)
                for s in range(1, n_dp)
            ]
            terms = [to_part(terms[s - 1], s) for s in range(1, n_dp)]
            total = contract_first(cols(left_side, 0), right_side)
            for term in terms:
                total = total + term.astype(jnp.float32)
            return transpose(total.astype(jnp.bfloat16))[None]

        down_proj_grad = weight_grad(grad_in, hidden)
        gate_proj_grad = weight_grad(expert_rows, grad_gate)
        up_proj_grad = weight_grad(expert_rows, grad_up)

        def join(left_side, right_side):
            part = contract_first(left_side, right_side)
            own, other = part[:token_count], part[token_count:].astype(jnp.bfloat16)
            other = across(other)
            return turn((own + other.astype(jnp.float32)).astype(jnp.bfloat16))

        layer_out = join(weighted, returned)
        tokens_grad = join(placing, grad_back)
        inner = contract_last(returned, og_two)
        routing = jnp.stack([jnp.sum(jnp.where(hit, inner, 0.0), axis=0) for hit in hits])
        routing_grad = (routing[:, :token_count] + across(routing[:, token_count:])).T
        return (layer_out, tokens_grad, routing_grad, gate_proj_grad, up_proj_grad, down_proj_grad)

    return body


def solution(mesh):
    in_specs = (
        P(("dp", "expert"), None),
        P(("dp", "expert"), None),
        P(("dp", "expert"), None),
        P(),
        P("expert", "dp", None),
        P("expert", "dp", None),
        P("expert", "dp", None),
        P(("dp", "expert"), None),
    )
    out_specs = (
        P(("dp", "expert"), None),
        P(("dp", "expert"), None),
        P(("dp", "expert"), None),
        P("expert", "dp", None),
        P("expert", "dp", None),
        P("expert", "dp", None),
    )
    body = make_body(mesh.shape["dp"], mesh.shape["expert"])
    return jax.shard_map(body, mesh=mesh, in_specs=in_specs, out_specs=out_specs, check_vma=False)
```

```python
import jax
import jax.numpy as jnp
import numpy as np
from jax import lax
from jax.sharding import PartitionSpec as P


TOPK = 2
AXES = ("dp", "expert")


def contract_last(left_side, right_side):
    return lax.dot_general(
        left_side, right_side, (((1,), (1,)), ((), ())), preferred_element_type=jnp.float32
    )


def contract_first(left_side, right_side):
    return lax.dot_general(
        left_side, right_side, (((0,), (0,)), ((), ())), preferred_element_type=jnp.float32
    )


def dot(left_side, right_side):
    return jnp.dot(left_side, right_side, preferred_element_type=jnp.float32)


def make_body(n_dp, n_ex):
    def physical(v, e):
        return ((v >> 1) * 2 + (e & 1)) * n_ex + (e >> 1) * 2 + (v & 1)

    def move(value, where):
        pairs = [
            (physical(v, e), physical(*where(v, e))) for v in range(n_dp) for e in range(n_ex)
        ]
        return lax.ppermute(value, AXES, pairs)

    def transpose(value):
        pairs = [
            (i * n_ex + c, ((i & ~1) | (c & 1)) * n_ex + ((c & ~1) | (i & 1)))
            for i in range(n_dp)
            for c in range(n_ex)
            if (i & 1) != (c & 1)
        ]
        moved = lax.ppermute(value, AXES, pairs)
        stays = (lax.axis_index("dp") & 1) == (lax.axis_index("expert") & 1)
        return lax.optimization_barrier(jnp.where(stays, value, moved))

    half = n_ex // 2

    def across(value, mask):
        return move(value, lambda v, e: (v, e ^ mask))

    def to_owner(value, d):
        return move(value, lambda v, e: (v, e ^ d))

    def to_part(value, s):
        return move(value, lambda v, e: (v ^ s, e))

    def body(
        tokens, gate_weights, expert_ids, hot_experts, gate_proj, up_proj, down_proj, out_grad
    ):
        token_count, model_width = tokens.shape
        width = model_width // n_dp
        assign_count = token_count * TOPK
        cap_rows = 5 * assign_count // (4 * n_ex)
        slot_count = cap_rows + assign_count // (2 * n_ex)
        i_index = lax.axis_index("dp")
        c_index = lax.axis_index("expert")
        v_index = (i_index >> 1) * 2 + (c_index & 1)
        e_index = (c_index >> 1) * 2 + (i_index & 1)

        def turned(value):
            blocks = [value[:, s * width : (s + 1) * width] for s in range(n_dp)]
            result = []
            for s in range(n_dp):
                pick = blocks[s]
                for j in range(n_dp):
                    if j != s:
                        pick = jnp.where(v_index == (j ^ s), blocks[j], pick)
                result.append(pick)
            return result

        own_routes = jnp.concatenate([expert_ids.T.astype(jnp.float32), gate_weights.T], axis=0)
        tok_routes = across(own_routes, half)
        og_routes = across(own_routes, 1)
        tok_far = across(tokens, half)
        og_far = across(out_grad, 1)
        tok_own, tok_far = turned(tokens), turned(tok_far)
        og_own, og_far = turned(out_grad), turned(og_far)

        def gathered(shard):
            own = transpose(shard[0])
            return [own] + [to_part(own, s) for s in range(1, n_dp)]

        gate_parts = gathered(gate_proj)
        up_parts = gathered(up_proj)
        down_parts = gathered(down_proj)

        def slots(ids):
            flat_ids = ids.reshape(ids.shape[0], -1)
            order = (
                jnp.arange(token_count, dtype=jnp.int32)[None, :] * TOPK
                + jnp.arange(TOPK, dtype=jnp.int32)[:, None]
            ).reshape(-1)
            same = (flat_ids[:, :, None] == flat_ids[:, None, :]) & (
                order[:, None] < order[None, :]
            )
            slot_pos = jnp.sum(same.astype(jnp.int32), axis=1)
            hot_row = jnp.any(flat_ids[:, None, :] == hot_experts[None, :, None], axis=1)
            kept_mask = slot_pos < jnp.where(hot_row, slot_count, cap_rows)
            return jnp.where(kept_mask, flat_ids * slot_count + slot_pos, -1).reshape(ids.shape)

        routes = jnp.stack([own_routes, tok_routes, og_routes])
        codes = slots(routes[:, :TOPK].astype(jnp.int32))

        def pairing(mask):
            steps = [d for d in range(n_ex) if not d & mask]
            row_d = np.repeat(np.array(steps, np.int32), 2 * slot_count)
            row_block = np.tile(np.repeat(np.arange(2, dtype=np.int32), slot_count), len(steps))
            row_slot = np.tile(np.arange(slot_count, dtype=np.int32), 2 * len(steps))
            code = (e_index ^ jnp.asarray(row_d)) * slot_count + jnp.asarray(row_slot)
            return steps, [jnp.where(jnp.asarray(row_block) == j, code, -2) for j in range(2)]

        def hits_of(row_code, code):
            return [row_code[:, None] == code[k][None, :] for k in range(TOPK)]

        def place_of(row_code, code):
            hits = hits_of(row_code, code)
            return (hits[0] | hits[1]).astype(jnp.bfloat16)

        def scaled_of(row_code, code, weights):
            hits = hits_of(row_code, code)
            return jnp.where(
                hits[0], weights[0][None, :], jnp.where(hits[1], weights[1][None, :], 0.0)
            )

        tok_steps, tok_rows_of = pairing(half)
        og_steps, og_rows_of = pairing(1)
        tok_codes = [codes[0], codes[1]]
        og_codes = [codes[0], codes[2]]
        tok_place = [place_of(tok_rows_of[j], tok_codes[j]) for j in range(2)]
        og_place = [place_of(og_rows_of[j], og_codes[j]) for j in range(2)]
        scaled = [scaled_of(og_rows_of[j], og_codes[j], routes[2 * j, TOPK:]) for j in range(2)]
        row_weight = jnp.sum(scaled[0] + scaled[1], axis=1, keepdims=True)
        weighted = [part.astype(jnp.bfloat16) for part in scaled]
        tok_place, og_place, weighted, row_weight = lax.optimization_barrier(
            (tok_place, og_place, weighted, row_weight)
        )
        swap = np.array([q // 2 + (q % 2) * half for q in range(n_ex)])
        old_row = (swap[:, None] * slot_count + np.arange(slot_count)[None, :]).reshape(-1)
        row_range = jnp.arange(n_ex * slot_count, dtype=jnp.int32)
        reorder = lax.optimization_barrier(
            (jnp.asarray(old_row, jnp.int32)[:, None] == row_range[None, :]).astype(jnp.bfloat16)
        )

        chunk = 2 * slot_count

        def exchange(rows, steps):
            pieces = [rows[j * chunk : (j + 1) * chunk] for j in range(half)]
            moved = [to_owner(pieces[j], steps[j]) for j in range(1, half)]
            return jnp.concatenate([pieces[0]] + moved, axis=0)

        tok_first = [dot(tok_place[0], part) for part in tok_own]
        og_first = [dot(og_place[0], part) for part in og_own]
        tok_rows = jnp.concatenate(
            [
                (tok_first[s] + dot(tok_place[1], tok_far[s])).astype(jnp.bfloat16)
                for s in range(n_dp)
            ],
            axis=1,
        )
        og_rows = jnp.concatenate(
            [
                (row_weight * (og_first[s] + dot(og_place[1], og_far[s]))).astype(jnp.bfloat16)
                for s in range(n_dp)
            ],
            axis=1,
        )
        expert_rows = exchange(tok_rows, tok_steps)
        grad_in = exchange(og_rows, og_steps)
        grad_in = dot(reorder, grad_in).astype(jnp.bfloat16)

        def cols(value, s):
            return value[:, s * width : (s + 1) * width]

        def through(value, parts):
            total = dot(cols(value, 0), parts[0])
            for s in range(1, n_dp):
                total = total + dot(cols(value, s), parts[s])
            return total

        gate_act = through(expert_rows, gate_parts)
        up_act = through(expert_rows, up_parts)
        hidden = (gate_act * jax.nn.sigmoid(gate_act) * up_act).astype(jnp.bfloat16)
        gate_act, up_act, hidden = lax.optimization_barrier((gate_act, up_act, hidden))
        output = jnp.concatenate(
            [contract_last(hidden, part).astype(jnp.bfloat16) for part in down_parts], axis=1
        )
        sigmoid_act = jax.nn.sigmoid(gate_act)
        silu_act = gate_act * sigmoid_act
        output = contract_first(reorder, output).astype(jnp.bfloat16)
        returned = exchange(output, og_steps)

        grad_hidden = through(grad_in, down_parts)
        grad_up = (grad_hidden * silu_act).astype(jnp.bfloat16)
        grad_gate = (
            grad_hidden * up_act * sigmoid_act * (1.0 + gate_act * (1.0 - sigmoid_act))
        ).astype(jnp.bfloat16)
        grad_rows = jnp.concatenate(
            [
                (
                    contract_last(grad_gate, gate_parts[s])
                    + contract_last(grad_up, up_parts[s])
                ).astype(jnp.bfloat16)
                for s in range(n_dp)
            ],
            axis=1,
        )
        grad_back = exchange(grad_rows, tok_steps)

        def weight_grad(left_side, right_side):
            terms = [
                contract_first(cols(left_side, s), right_side).astype(jnp.bfloat16)
                for s in range(1, n_dp)
            ]
            terms = [to_part(terms[s - 1], s) for s in range(1, n_dp)]
            total = contract_first(cols(left_side, 0), right_side)
            for term in terms:
                total = total + term.astype(jnp.float32)
            return transpose(total.astype(jnp.bfloat16))[None]

        down_proj_grad = weight_grad(grad_in, hidden)
        gate_proj_grad = weight_grad(expert_rows, grad_gate)
        up_proj_grad = weight_grad(expert_rows, grad_up)

        def join(sides, right_side, mask):
            other = contract_first(sides[1], right_side).astype(jnp.bfloat16)
            other = across(other, mask)
            own = contract_first(sides[0], right_side)
            total = (own + other.astype(jnp.float32)).astype(jnp.bfloat16)
            return jnp.concatenate(turned(total), axis=1)

        layer_out = join(weighted, returned, 1)
        tokens_grad = join(tok_place, grad_back, half)
        late_codes, late_rows, _ = lax.optimization_barrier((og_codes, og_rows_of, returned))

        def inner_sums(og_parts, j):
            inner = contract_last(cols(returned, 0), og_parts[0])
            for s in range(1, n_dp):
                inner = inner + contract_last(cols(returned, s), og_parts[s])
            hits = hits_of(late_rows[j], late_codes[j])
            return jnp.stack([jnp.sum(jnp.where(hit, inner, 0.0), axis=0) for hit in hits])

        routing_far = inner_sums(og_far, 1)
        routing_far = across(routing_far, 1)
        routing_grad = (inner_sums(og_own, 0) + routing_far).T
        return (layer_out, tokens_grad, routing_grad, gate_proj_grad, up_proj_grad, down_proj_grad)

    return body


def solution(mesh):
    in_specs = (
        P(("dp", "expert"), None),
        P(("dp", "expert"), None),
        P(("dp", "expert"), None),
        P(),
        P("expert", "dp", None),
        P("expert", "dp", None),
        P("expert", "dp", None),
        P(("dp", "expert"), None),
    )
    out_specs = (
        P(("dp", "expert"), None),
        P(("dp", "expert"), None),
        P(("dp", "expert"), None),
        P("expert", "dp", None),
        P("expert", "dp", None),
        P("expert", "dp", None),
    )
    body = make_body(mesh.shape["dp"], mesh.shape["expert"])
    return jax.shard_map(body, mesh=mesh, in_specs=in_specs, out_specs=out_specs, check_vma=False)
```

```python
import jax
import jax.numpy as jnp
import numpy as np
from jax import lax
from jax.sharding import PartitionSpec as P


TOPK = 2
AXES = ("dp", "expert")


def contract_last(left_side, right_side):
    return lax.dot_general(
        left_side, right_side, (((1,), (1,)), ((), ())), preferred_element_type=jnp.float32
    )


def contract_first(left_side, right_side):
    return lax.dot_general(
        left_side, right_side, (((0,), (0,)), ((), ())), preferred_element_type=jnp.float32
    )


def dot(left_side, right_side):
    return jnp.dot(left_side, right_side, preferred_element_type=jnp.float32)


def make_body(n_dp, n_ex):
    def physical(v, e):
        return ((v >> 1) * 2 + (e & 1)) * n_ex + (e >> 1) * 2 + (v & 1)

    def move(value, where):
        pairs = [
            (physical(v, e), physical(*where(v, e))) for v in range(n_dp) for e in range(n_ex)
        ]
        return lax.ppermute(value, AXES, pairs)

    def transpose(value):
        pairs = [
            (i * n_ex + c, ((i & ~1) | (c & 1)) * n_ex + ((c & ~1) | (i & 1)))
            for i in range(n_dp)
            for c in range(n_ex)
            if (i & 1) != (c & 1)
        ]
        moved = lax.ppermute(value, AXES, pairs)
        stays = (lax.axis_index("dp") & 1) == (lax.axis_index("expert") & 1)
        return lax.optimization_barrier(jnp.where(stays, value, moved))

    half = n_ex // 2

    def across(value, mask):
        return move(value, lambda v, e: (v, e ^ mask))

    def to_owner(value, d):
        return move(value, lambda v, e: (v, e ^ d))

    def to_part(value, s):
        return move(value, lambda v, e: (v ^ s, e))

    def body(
        tokens, gate_weights, expert_ids, hot_experts, gate_proj, up_proj, down_proj, out_grad
    ):
        token_count, model_width = tokens.shape
        width = model_width // n_dp
        assign_count = token_count * TOPK
        cap_rows = 5 * assign_count // (4 * n_ex)
        slot_count = cap_rows + assign_count // (2 * n_ex)
        i_index = lax.axis_index("dp")
        c_index = lax.axis_index("expert")
        v_index = (i_index >> 1) * 2 + (c_index & 1)
        e_index = (c_index >> 1) * 2 + (i_index & 1)

        def turned(value):
            blocks = [value[:, s * width : (s + 1) * width] for s in range(n_dp)]
            result = []
            for s in range(n_dp):
                pick = blocks[s]
                for j in range(n_dp):
                    if j != s:
                        pick = jnp.where(v_index == (j ^ s), blocks[j], pick)
                result.append(pick)
            return result

        own_routes = jnp.concatenate([expert_ids.T.astype(jnp.float32), gate_weights.T], axis=0)
        tok_routes = across(own_routes, half)
        og_routes = across(own_routes, 1)
        tok_far = across(tokens, half)
        og_far = across(out_grad, 1)
        tok_own, tok_far = turned(tokens), turned(tok_far)
        og_own, og_far = turned(out_grad), turned(og_far)

        def gathered(shard):
            own = transpose(shard[0])
            return [own] + [to_part(own, s) for s in range(1, n_dp)]

        gate_parts = gathered(gate_proj)
        up_parts = gathered(up_proj)
        down_parts = gathered(down_proj)

        def slots(ids):
            flat_ids = ids.reshape(ids.shape[0], -1)
            order = (
                jnp.arange(token_count, dtype=jnp.int32)[None, :] * TOPK
                + jnp.arange(TOPK, dtype=jnp.int32)[:, None]
            ).reshape(-1)
            same = (flat_ids[:, :, None] == flat_ids[:, None, :]) & (
                order[:, None] < order[None, :]
            )
            slot_pos = jnp.sum(same.astype(jnp.int32), axis=1)
            hot_row = jnp.any(flat_ids[:, None, :] == hot_experts[None, :, None], axis=1)
            kept_mask = slot_pos < jnp.where(hot_row, slot_count, cap_rows)
            return jnp.where(kept_mask, flat_ids * slot_count + slot_pos, -1).reshape(ids.shape)

        routes = jnp.stack([own_routes, tok_routes, og_routes])
        codes = slots(routes[:, :TOPK].astype(jnp.int32))

        def pairing(mask):
            steps = [d for d in range(n_ex) if not d & mask]
            row_d = np.repeat(np.array(steps, np.int32), 2 * slot_count)
            row_block = np.tile(np.repeat(np.arange(2, dtype=np.int32), slot_count), len(steps))
            row_slot = np.tile(np.arange(slot_count, dtype=np.int32), 2 * len(steps))
            code = (e_index ^ jnp.asarray(row_d)) * slot_count + jnp.asarray(row_slot)
            return steps, [jnp.where(jnp.asarray(row_block) == j, code, -2) for j in range(2)]

        def hits_of(row_code, code):
            return [row_code[:, None] == code[k][None, :] for k in range(TOPK)]

        def place_of(row_code, code):
            hits = hits_of(row_code, code)
            return (hits[0] | hits[1]).astype(jnp.bfloat16)

        def scaled_of(row_code, code, weights):
            hits = hits_of(row_code, code)
            return jnp.where(
                hits[0], weights[0][None, :], jnp.where(hits[1], weights[1][None, :], 0.0)
            )

        tok_steps, tok_rows_of = pairing(half)
        og_steps, og_rows_of = pairing(1)
        tok_codes = [codes[0], codes[1]]
        og_codes = [codes[0], codes[2]]
        tok_place = [place_of(tok_rows_of[j], tok_codes[j]) for j in range(2)]
        og_place = [place_of(og_rows_of[j], og_codes[j]) for j in range(2)]
        scaled = [scaled_of(og_rows_of[j], og_codes[j], routes[2 * j, TOPK:]) for j in range(2)]
        row_weight = jnp.sum(scaled[0] + scaled[1], axis=1, keepdims=True)
        weighted = [part.astype(jnp.bfloat16) for part in scaled]
        tok_place, og_place, weighted, row_weight = lax.optimization_barrier(
            (tok_place, og_place, weighted, row_weight)
        )
        swap = np.array([q // 2 + (q % 2) * half for q in range(n_ex)])
        old_row = (swap[:, None] * slot_count + np.arange(slot_count)[None, :]).reshape(-1)
        row_range = jnp.arange(n_ex * slot_count, dtype=jnp.int32)
        reorder = lax.optimization_barrier(
            (jnp.asarray(old_row, jnp.int32)[:, None] == row_range[None, :]).astype(jnp.bfloat16)
        )

        chunk = 2 * slot_count

        def exchange(rows, steps):
            pieces = [rows[j * chunk : (j + 1) * chunk] for j in range(half)]
            moved = []
            for j in range(1, half):
                moved.append(to_owner(pieces[j], steps[j]))
            return jnp.concatenate([pieces[0]] + moved, axis=0)

        tok_first = [dot(tok_place[0], part) for part in tok_own]
        og_first = [dot(og_place[0], part) for part in og_own]
        tok_rows = jnp.concatenate(
            [
                (tok_first[s] + dot(tok_place[1], tok_far[s])).astype(jnp.bfloat16)
                for s in range(n_dp)
            ],
            axis=1,
        )
        og_rows = jnp.concatenate(
            [
                (row_weight * (og_first[s] + dot(og_place[1], og_far[s]))).astype(jnp.bfloat16)
                for s in range(n_dp)
            ],
            axis=1,
        )
        expert_rows = exchange(tok_rows, tok_steps)
        grad_in = exchange(og_rows, og_steps)
        grad_in = dot(reorder, grad_in).astype(jnp.bfloat16)

        def cols(value, s):
            return value[:, s * width : (s + 1) * width]

        def through(value, parts):
            total = dot(cols(value, 0), parts[0])
            for s in range(1, n_dp):
                total = total + dot(cols(value, s), parts[s])
            return total

        gate_act = through(expert_rows, gate_parts)
        up_act = through(expert_rows, up_parts)
        hidden = (gate_act * jax.nn.sigmoid(gate_act) * up_act).astype(jnp.bfloat16)
        gate_act, up_act, hidden = lax.optimization_barrier((gate_act, up_act, hidden))
        output = jnp.concatenate(
            [contract_last(hidden, part).astype(jnp.bfloat16) for part in down_parts], axis=1
        )
        sigmoid_act = jax.nn.sigmoid(gate_act)
        silu_act = gate_act * sigmoid_act
        output = contract_first(reorder, output).astype(jnp.bfloat16)
        returned = exchange(output, og_steps)

        grad_hidden = through(grad_in, down_parts)
        grad_up = (grad_hidden * silu_act).astype(jnp.bfloat16)
        grad_gate = (
            grad_hidden * up_act * sigmoid_act * (1.0 + gate_act * (1.0 - sigmoid_act))
        ).astype(jnp.bfloat16)
        grad_rows = jnp.concatenate(
            [
                (
                    contract_last(grad_gate, gate_parts[s])
                    + contract_last(grad_up, up_parts[s])
                ).astype(jnp.bfloat16)
                for s in range(n_dp)
            ],
            axis=1,
        )
        grad_back = exchange(grad_rows, tok_steps)

        def weight_grad(left_side, right_side):
            terms = [
                contract_first(cols(left_side, s), right_side).astype(jnp.bfloat16)
                for s in range(1, n_dp)
            ]
            terms = [to_part(terms[s - 1], s) for s in range(1, n_dp)]
            total = contract_first(cols(left_side, 0), right_side)
            for term in terms:
                total = total + term.astype(jnp.float32)
            return transpose(total.astype(jnp.bfloat16))[None]

        down_proj_grad = weight_grad(grad_in, hidden)
        gate_proj_grad = weight_grad(expert_rows, grad_gate)
        up_proj_grad = weight_grad(expert_rows, grad_up)

        def join(sides, right_side, mask):
            other = contract_first(sides[1], right_side).astype(jnp.bfloat16)
            other = across(other, mask)
            own = contract_first(sides[0], right_side)
            total = (own + other.astype(jnp.float32)).astype(jnp.bfloat16)
            total = lax.optimization_barrier(total)
            return jnp.concatenate(turned(total), axis=1)

        layer_out = join(weighted, returned, 1)
        tokens_grad = join(tok_place, grad_back, half)
        late_codes, late_rows, _ = lax.optimization_barrier((og_codes, og_rows_of, returned))

        def inner_sums(og_parts, j):
            inner = contract_last(cols(returned, 0), og_parts[0])
            for s in range(1, n_dp):
                inner = inner + contract_last(cols(returned, s), og_parts[s])
            hits = hits_of(late_rows[j], late_codes[j])
            return jnp.stack([jnp.sum(jnp.where(hit, inner, 0.0), axis=0) for hit in hits])

        routing_far = inner_sums(og_far, 1)
        routing_far = across(routing_far, 1)
        routing_grad = (inner_sums(og_own, 0) + routing_far).T
        return (layer_out, tokens_grad, routing_grad, gate_proj_grad, up_proj_grad, down_proj_grad)

    return body


def solution(mesh):
    in_specs = (
        P(("dp", "expert"), None),
        P(("dp", "expert"), None),
        P(("dp", "expert"), None),
        P(),
        P("expert", "dp", None),
        P("expert", "dp", None),
        P("expert", "dp", None),
        P(("dp", "expert"), None),
    )
    out_specs = (
        P(("dp", "expert"), None),
        P(("dp", "expert"), None),
        P(("dp", "expert"), None),
        P("expert", "dp", None),
        P("expert", "dp", None),
        P("expert", "dp", None),
    )
    body = make_body(mesh.shape["dp"], mesh.shape["expert"])
    return jax.shard_map(body, mesh=mesh, in_specs=in_specs, out_specs=out_specs, check_vma=False)
```
